32 devices in a mesh: grp: 2 (over x), tm: 8 (over z, y), head: 2 (over core).
Axes of the slice: x: 2, y: 2, z: 4, core: 2. Of those that a mesh axis runs over, the one named last changes fastest.
Arguments:
- queries: bfloat16 [2048, 6144], P(('grp', 'tm'), 'head'), parts along dimension 0, may hold values from -130 to 130
- keys: bfloat16 [2048, 1024], P(('grp', 'tm'), 'head'), parts along dimension 0, may hold values from -7 to 7
- values: bfloat16 [2048, 1024], P(('grp', 'tm'), 'head'), parts along dimension 0, may hold values from -6 to 6
- span_mask: int32 [8, 4], P('grp'), parts along dimension 0, may hold values from 0 to 1, as said below
- section: int32 [8], P('grp'), parts along dimension 0, may hold values from 0 to 3
- section_gate: float32 [4, 6144], P(None, 'head'), may hold values from 0.1 to 1.9
Outputs:
- mixed: bfloat16 [2048, 6144], P(('grp', 'tm'), 'head'), parts along dimension 0
- log_total: float32 [48, 2048], P('head', ('grp', 'tm')), parts along dimension 1
The draws below stay inside these ranges and needn't reach their ends.
There are 2 independent parts, one for each index of `grp`. The reference program is written for one: setup_inputs(seed, part) draws one part's arguments, and reference() takes and returns one part's arrays. A program takes and returns all parts, laid end to end along the dimension named above; an argument that names none is the same for every part. Nothing has to cross between parts.
Inputs may be any that keep to these rules, and one draw needn't show every extreme that they name: `span_mask`: the first column and the diagonal are 1 and everything above the diagonal is 0.
All inputs are finite; a program needn't handle non-finite values.
Results may differ from the reference program's by a relative error of at most 0.006.
Values may be sent and summed in bfloat16 or wider, within the bound.
A program may use at most 64 MiB of HBM per device.

```python
import math
import jax
import jax.numpy as jnp
from jax import lax

QUERY_HEADS = 48
KEY_VALUE_HEADS = 8
HEAD_SIZE = 128
CH = 256
SECTIONS = 4
CLIP_TOKENS = 1024
NC = 4


def paired_fields(key):
    base = jax.random.fold_in(key, 7)
    random_key_first, key_b = jax.random.split(base, 2)
    keys_float = jnp.clip(jax.random.normal(random_key_first, (CLIP_TOKENS, KEY_VALUE_HEADS * HEAD_SIZE), jnp.float32), -6.0, 6.0)
    queries_f = 2.0 * jnp.clip(jax.random.normal(key_b, (CLIP_TOKENS, QUERY_HEADS * HEAD_SIZE), jnp.float32), -6.0, 6.0)
    return (queries_f, keys_float)


def draw_queries(key, part):
    return paired_fields(key)[0].astype(jnp.bfloat16)


def draw_keys(key, part):
    return paired_fields(key)[1].astype(jnp.bfloat16)


def draw_span_mask(key, part):
    coin = jax.random.randint(jax.random.fold_in(key, 11), (NC, NC), 0, 2)
    row_ids = jnp.arange(NC, dtype=jnp.int32)[:, None]
    col_ids = jnp.arange(NC, dtype=jnp.int32)[None, :]
    result = jnp.where(col_ids < row_ids, coin, 0)
    result = jnp.where(col_ids == row_ids, 1, result)
    result = jnp.where(col_ids == 0, 1, result)
    return result.astype(jnp.int32)


def touch_ends(drawn, stream_key, low, largest):
    dims = drawn.shape
    place = [jax.random.randint(jax.random.fold_in(stream_key, axis), (), 0, dims[axis]) for axis in range(len(dims))]
    drawn = drawn.at[tuple(place)].set(low)
    longest = dims.index(max(dims))
    place[longest] = (place[longest] + 1) % dims[longest]
    return drawn.at[tuple(place)].set(largest)


def block_scale(own_key, shape, shards, least, high):
    factor_of, own = 1.0, jax.random.fold_in(own_key, 6)
    for axis_at, parts in shards:
        heights = jnp.exp(jax.random.uniform(jax.random.fold_in(own, axis_at), (parts,), jnp.float32, least / len(shards), high / len(shards)))
        factor_of = factor_of * jnp.repeat(heights, shape[axis_at] // parts).reshape([-1 if axis == axis_at else 1 for axis in range(len(shape))])
    return factor_of


def scatter_about(stream_key, dims, deviation, most, shards=(), held_as=jnp.bfloat16):
    entries = deviation * jax.random.normal(stream_key, dims, jnp.float32)
    if shards:
        entries = entries * block_scale(stream_key, dims, shards, -0.22, 0.18)
    return jnp.clip(entries, -most, most).astype(held_as)


def setup_inputs(seed: int = 0, part: int = 0) -> dict:
    arg_keys = jax.random.split(jax.random.key(seed), 7)
    own_keys = jax.random.split(jax.random.fold_in(arg_keys[6], part), 7)
    queries = draw_queries(jax.random.fold_in(jax.random.fold_in(arg_keys[6], part), 71), part)
    keys = draw_keys(jax.random.fold_in(jax.random.fold_in(arg_keys[6], part), 71), part)
    values = scatter_about(own_keys[2], (CLIP_TOKENS, KEY_VALUE_HEADS * HEAD_SIZE), 1.0, 6.0, ((0, 8), (1, 2)))
    span_mask = draw_span_mask(jax.random.fold_in(jax.random.fold_in(arg_keys[6], part), 71), part)
    section = touch_ends(jax.random.randint(own_keys[4], (NC,), 0, SECTIONS), jax.random.fold_in(own_keys[4], 1), 0, SECTIONS - 1).astype(jnp.int32)
    section_gate = jnp.clip(1.0 + 0.18 * jax.random.normal(arg_keys[5], (SECTIONS, QUERY_HEADS * HEAD_SIZE), jnp.float32), 0.1, 1.9)
    return dict(queries=queries, keys=keys, values=values, span_mask=span_mask, section=section, section_gate=section_gate)


def reference(queries, keys, values, span_mask, section, section_gate):
    total_rows = queries.shape[0]
    query_group = QUERY_HEADS // KEY_VALUE_HEADS
    span_ids = (jnp.arange(total_rows, dtype=jnp.int32) // CH).astype(jnp.int32)
    allowed = jnp.take(jnp.take(span_mask, span_ids, axis=0), span_ids, axis=1) > 0
    scale = 1.0 / math.sqrt(HEAD_SIZE)

    def one_head(head_index):
        start_q = (head_index * HEAD_SIZE).astype(jnp.int32)
        start_k = (head_index // query_group * HEAD_SIZE).astype(jnp.int32)
        query_head = lax.dynamic_slice_in_dim(queries, start_q, HEAD_SIZE, 1)
        key_head = lax.dynamic_slice_in_dim(keys, start_k, HEAD_SIZE, 1)
        value_head = lax.dynamic_slice_in_dim(values, start_k, HEAD_SIZE, 1)
        score = jnp.dot(query_head, key_head.T, preferred_element_type=jnp.float32) * scale
        score = jnp.where(allowed, score, -1e+30)
        top = lax.optimization_barrier(jnp.max(score, axis=1))
        weight = jnp.where(allowed, jnp.exp(score - top[:, None]), 0.0)
        total = lax.optimization_barrier(jnp.sum(weight, axis=1))
        attended = jnp.dot(weight.astype(jnp.bfloat16), value_head, preferred_element_type=jnp.float32) / total[:, None]
        return (attended, top + jnp.log(total))
    attended, log_total = lax.map(one_head, jnp.arange(QUERY_HEADS, dtype=jnp.int32))
    attended = jnp.transpose(attended, (1, 0, 2)).reshape(total_rows, QUERY_HEADS * HEAD_SIZE)
    gate_rows = jnp.take(section_gate, jnp.take(section, span_ids), axis=0)
    mixed = (gate_rows * attended).astype(jnp.bfloat16)
    return (mixed, log_total)
```

```python
import functools
import math

import jax
import jax.numpy as jnp
from jax import lax
from jax.experimental import pallas as pl
from jax.experimental.pallas import tpu as pltpu
from jax.sharding import PartitionSpec as P

HEAD_SIZE = 128
CH = 256
MESH = pl.DeviceIdType.MESH
LOG2E = 1.4426950408889634
LN2 = 0.6931471805599453
FAR = 1e30


def kernel(
    count, chunks, q_hbm, k_hbm, v_hbm, mask_ref, sec_ref, gate_ref, out_ref, lt_ref,
    qbuf, kbuf, vbuf, top_s, tot_s, acc_s, ltm_s, gate_s, qsem, ksem, vsem,
    krecv, vrecv, kz, vz, ky, vy,
):
    q_heads, rows = qbuf.shape[0], qbuf.shape[1]
    kv_heads = kbuf.shape[1]
    group = q_heads // kv_heads
    per = kv_heads // chunks
    pairs = count // 2
    factor = LOG2E / math.sqrt(HEAD_SIZE)

    me = lax.axis_index("tm")
    pair = me // 2
    side = me % 2
    partner = me + 1 - 2 * side
    has_prev = pair > 0
    has_next = pair < pairs - 1

    def head_copy(src, dst, sem, head):
        return pltpu.make_async_copy(
            src.at[:, pl.ds(head * HEAD_SIZE, HEAD_SIZE)], dst, sem
        )

    own_k = [head_copy(k_hbm, kbuf.at[me, h], ksem.at[h], h) for h in range(kv_heads)]
    own_v = [head_copy(v_hbm, vbuf.at[me, h], vsem.at[h], h) for h in range(kv_heads)]
    own_q = [head_copy(q_hbm, qbuf.at[h], qsem.at[h], h) for h in range(q_heads)]
    for copy in own_k + own_v:
        copy.start()

    barrier = pltpu.get_barrier_semaphore()
    pl.semaphore_signal(barrier, inc=1, device_id={"tm": partner}, device_id_type=MESH)

    @pl.when(has_next)
    def _():
        pl.semaphore_signal(barrier, inc=1, device_id={"tm": me + 2}, device_id_type=MESH)

    @pl.when(has_prev)
    def _():
        pl.semaphore_signal(barrier, inc=1, device_id={"tm": me - 2}, device_id_type=MESH)

    for copy in own_q:
        copy.start()
    pl.semaphore_wait(
        barrier, 1 + has_next.astype(jnp.int32) + has_prev.astype(jnp.int32)
    )

    def send(buf, send_sem, recv_sem, slot, c, target):
        piece = buf.at[slot, pl.ds(c * per, per)]
        return pltpu.make_async_remote_copy(
            src_ref=piece,
            dst_ref=piece,
            send_sem=send_sem.at[slot, c],
            recv_sem=recv_sem.at[slot, c],
            device_id={"tm": target},
            device_id_type=MESH,
        )

    def k_on(slot, c):
        return send(kbuf, kz, krecv, slot, c, me + 2)

    def v_on(slot, c):
        return send(vbuf, vz, vrecv, slot, c, me + 2)

    def k_over(slot, c):
        return send(kbuf, ky, krecv, slot, c, partner)

    def v_over(slot, c):
        return send(vbuf, vy, vrecv, slot, c, partner)

    for c in range(chunks):
        for h in range(c * per, (c + 1) * per):
            own_k[h].wait()

        @pl.when(has_next)
        def _():
            k_on(me, c).start()

        k_over(me, c).start()
        for h in range(c * per, (c + 1) * per):
            own_v[h].wait()

        @pl.when(has_next)
        def _():
            v_on(me, c).start()

        v_over(me, c).start()

    def visit(slots, first, last):
        allowed = [mask_ref[pair, slot // 2] > 0 for slot in slots]

        def one(head, carry):
            keys = jnp.concatenate([kbuf[slot, head] for slot in slots], axis=0)
            vals = jnp.concatenate([vbuf[slot, head] for slot in slots], axis=0)
            for g in range(group):
                j = head * group + g
                score = factor * lax.dot_general(
                    qbuf[j], keys, (((1,), (1,)), ((), ())),
                    preferred_element_type=jnp.float32,
                )
                parts = [score[:, i * rows:(i + 1) * rows] for i in range(len(slots))]
                tops = [
                    jnp.where(ok, jnp.max(part, axis=1, keepdims=True), -FAR)
                    for ok, part in zip(allowed, parts)
                ]
                top = functools.reduce(jnp.maximum, tops)
                if not first:
                    before = top_s[j]
                    top = jnp.maximum(before, top)
                top = jnp.broadcast_to(top, (rows, HEAD_SIZE))
                weights = [
                    jnp.exp2(part - jnp.where(ok, top, FAR))
                    for ok, part in zip(allowed, parts)
                ]
                total = functools.reduce(jnp.add, weights)
                weight = jnp.concatenate(
                    [w.astype(jnp.bfloat16) for w in weights], axis=1
                )
                acc = jnp.dot(weight, vals, preferred_element_type=jnp.float32)
                if not first:
                    fade = jnp.exp2(before - top)
                    total = total + tot_s[j] * fade
                    acc = acc + acc_s[j] * fade
                if last:
                    full = jnp.sum(total, axis=1, keepdims=True)
                    cols = pl.ds(pl.multiple_of(j * HEAD_SIZE, HEAD_SIZE), HEAD_SIZE)
                    gate = gate_s[:, cols]
                    out_ref[:, cols] = (gate * (acc / full)).astype(out_ref.dtype)
                    log_total = top * LN2 + jnp.log(full)
                    lane = lax.broadcasted_iota(jnp.int32, (rows, HEAD_SIZE), 1)
                    ltm_s[...] = jnp.where(lane == j, log_total, ltm_s[...])
                else:
                    top_s[j] = top
                    tot_s[j] = total
                    acc_s[j] = acc
            return carry

        lax.fori_loop(0, kv_heads, one, 0)

    for copy in own_q:
        copy.wait()
    visit([me], True, False)
    gate_row = gate_ref[pl.ds(0, 1), :]
    for i in range(1, gate_ref.shape[0]):
        gate_row = jnp.where(sec_ref[pair] == i, gate_ref[pl.ds(i, 1), :], gate_row)
    gate_s[...] = gate_row
    ltm_s[...] = jnp.zeros_like(ltm_s)

    def step(i, carry):
        behind = me - 2 * i
        across = partner - 2 * (i - 1)
        for c in range(chunks):
            k_on(behind, c).wait_recv()

            @pl.when(has_next)
            def _():
                k_on(behind, c).start()

            k_over(behind, c).start()
            v_on(behind, c).wait_recv()

            @pl.when(has_next)
            def _():
                v_on(behind, c).start()

            @pl.when(behind >= 2)
            def _():
                v_over(behind, c).start()

        for c in range(chunks):
            k_over(across, c).wait_recv()
            v_over(across, c).wait_recv()
        visit([behind, across], False, False)
        return carry

    lax.fori_loop(1, pair + 1, step, 0)

    far = 1 - side
    for c in range(chunks):
        v_on(far, c).wait_recv()

        @pl.when(has_next)
        def _():
            v_on(far, c).start()

    for c in range(chunks):
        k_over(far, c).wait_recv()
    visit([far], False, True)
    lt_ref[...] = jnp.transpose(ltm_s[...])[:q_heads]

    def settle(i, carry):
        slot = me - 2 * i
        for c in range(chunks):

            @pl.when(has_next)
            def _():
                k_on(slot, c).wait_send()
                v_on(slot, c).wait_send()

            k_over(slot, c).wait_send()

            @pl.when((slot >= 2) | (i == 0))
            def _():
                v_over(slot, c).wait_send()

        return carry

    lax.fori_loop(0, pair + 1, settle, 0)

    @pl.when(has_next)
    def _():
        for c in range(chunks):
            v_on(far, c).wait_send()


def solution(mesh):
    count = mesh.shape["tm"]

    def on_device(queries, keys, values, span_mask, section, section_gate):
        rows = queries.shape[0]
        q_heads = queries.shape[1] // HEAD_SIZE
        kv_heads = keys.shape[1] // HEAD_SIZE
        assert CH == 2 * rows and count % 2 == 0
        chunks = 2 if kv_heads % 2 == 0 else 1
        any_spec = pl.BlockSpec(memory_space=pl.ANY)
        smem = pl.BlockSpec(memory_space=pltpu.SMEM)
        vmem = pl.BlockSpec(memory_space=pltpu.VMEM)
        dma = pltpu.SemaphoreType.DMA
        state = pltpu.VMEM((q_heads, rows, HEAD_SIZE), jnp.float32)
        held = pltpu.VMEM((count, kv_heads, rows, HEAD_SIZE), jnp.bfloat16)
        return pl.pallas_call(
            functools.partial(kernel, count, chunks),
            out_shape=(
                jax.ShapeDtypeStruct(queries.shape, jnp.bfloat16),
                jax.ShapeDtypeStruct((q_heads, rows), jnp.float32),
            ),
            in_specs=[any_spec] * 3 + [smem, smem, vmem],
            out_specs=(vmem, vmem),
            scratch_shapes=[
                pltpu.VMEM((q_heads, rows, HEAD_SIZE), jnp.bfloat16),
                held, held, state, state, state,
                pltpu.VMEM((rows, HEAD_SIZE), jnp.float32),
                pltpu.VMEM((1, queries.shape[1]), jnp.float32),
                dma((q_heads,)), dma((kv_heads,)), dma((kv_heads,)),
            ] + [dma((count, chunks))] * 6,
            compiler_params=pltpu.CompilerParams(
                collective_id=0, has_side_effects=True, vmem_limit_bytes=40 * 2**20
            ),
            name="span_attention",
        )(queries, keys, values, span_mask, section, section_gate)

    placed = (
        P(("grp", "tm"), "head"),
        P(("grp", "tm"), "head"),
        P(("grp", "tm"), "head"),
        P("grp", None),
        P("grp"),
        P(None, "head"),
    )
    return jax.shard_map(
        on_device,
        mesh=mesh,
        in_specs=placed,
        out_specs=(P(("grp", "tm"), "head"), P("head", ("grp", "tm"))),
        check_vma=False,
    )
```

```python
import functools
import math

import jax
import jax.numpy as jnp
from jax import lax
from jax.experimental import pallas as pl
from jax.experimental.pallas import tpu as pltpu
from jax.sharding import PartitionSpec as P

HEAD_SIZE = 128
CH = 256
MESH = pl.DeviceIdType.MESH
LOG2E = 1.4426950408889634
LN2 = 0.6931471805599453
FAR = 1e30


def kernel(
    count, chunks, q_hbm, k_hbm, v_hbm, mask_hbm, sec_hbm, gate_hbm, out_ref, lt_ref,
    qbuf, kbuf, vbuf, top_s, tot_s, acc_s, ltm_s, gate_s, mask_ref, sec_ref, gate_ref, small, qsem, ksem, vsem,
    krecv, vrecv, kz, vz, ky, vy,
):
    q_heads, rows = qbuf.shape[0], qbuf.shape[1]
    kv_heads = kbuf.shape[1]
    group = q_heads // kv_heads
    per = kv_heads // chunks
    pairs = count // 2
    tile = group
    factor = LOG2E / math.sqrt(HEAD_SIZE)

    me = lax.axis_index("tm")
    pair = me // 2
    side = me % 2
    partner = me + 1 - 2 * side
    has_prev = pair > 0
    has_next = pair < pairs - 1

    def head_copy(src, dst, sem, head):
        return pltpu.make_async_copy(
            src.at[:, pl.ds(head * HEAD_SIZE, HEAD_SIZE)], dst, sem
        )

    own_k = [head_copy(k_hbm, kbuf.at[me, h], ksem.at[h], h) for h in range(kv_heads)]
    own_v = [head_copy(v_hbm, vbuf.at[me, h], vsem.at[h], h) for h in range(kv_heads)]
    own_q = [head_copy(q_hbm, qbuf.at[h], qsem.at[h], h) for h in range(q_heads)]
    for copy in own_k + own_v:
        copy.start()

    barrier = pltpu.get_barrier_semaphore()
    pl.semaphore_signal(barrier, inc=1, device_id={"tm": partner}, device_id_type=MESH)

    @pl.when(has_next)
    def _():
        pl.semaphore_signal(barrier, inc=1, device_id={"tm": me + 2}, device_id_type=MESH)

    @pl.when(has_prev)
    def _():
        pl.semaphore_signal(barrier, inc=1, device_id={"tm": me - 2}, device_id_type=MESH)

    own_small = [
        pltpu.make_async_copy(mask_hbm, mask_ref, small.at[0]),
        pltpu.make_async_copy(sec_hbm, sec_ref, small.at[1]),
        pltpu.make_async_copy(gate_hbm, gate_ref, small.at[2]),
    ]
    for copy in own_q + own_small:
        copy.start()
    pl.semaphore_wait(
        barrier, 1 + has_next.astype(jnp.int32) + has_prev.astype(jnp.int32)
    )

    def send(buf, send_sem, recv_sem, slot, c, target):
        piece = buf.at[slot, pl.ds(c * per, per)]
        return pltpu.make_async_remote_copy(
            src_ref=piece,
            dst_ref=piece,
            send_sem=send_sem.at[slot, c],
            recv_sem=recv_sem.at[slot, c],
            device_id={"tm": target},
            device_id_type=MESH,
        )

    def k_on(slot, c):
        return send(kbuf, kz, krecv, slot, c, me + 2)

    def v_on(slot, c):
        return send(vbuf, vz, vrecv, slot, c, me + 2)

    def k_over(slot, c):
        return send(kbuf, ky, krecv, slot, c, partner)

    def v_over(slot, c):
        return send(vbuf, vy, vrecv, slot, c, partner)

    for c in range(chunks):
        for h in range(c * per, (c + 1) * per):
            own_k[h].wait()

        @pl.when(has_next)
        def _():
            k_on(me, c).start()

        k_over(me, c).start()
        for h in range(c * per, (c + 1) * per):
            own_v[h].wait()

        @pl.when(has_next)
        def _():
            v_on(me, c).start()

        v_over(me, c).start()

    def visit(slots, head, first, last):
        allowed = [mask_ref[pair, slot // 2] > 0 for slot in slots]
        keys = jnp.concatenate([kbuf[slot, head] for slot in slots], axis=0)
        vals = jnp.concatenate([vbuf[slot, head] for slot in slots], axis=0)
        base = head * group
        tiles = range(0, group, tile)
        tall = tile * rows

        def held(ref, g):
            return ref[pl.ds(base + g, tile)].reshape(tall, HEAD_SIZE)

        def keep(ref, g, value):
            ref[pl.ds(base + g, tile)] = value.reshape(tile, rows, HEAD_SIZE)

        if not first:
            before = [held(top_s, g) for g in tiles]
            tot_old = [held(tot_s, g) for g in tiles]
            acc_old = [held(acc_s, g) for g in tiles]
        done = []
        for n, g in enumerate(tiles):
            score = factor * lax.dot_general(
                held(qbuf, g), keys, (((1,), (1,)), ((), ())),
                preferred_element_type=jnp.float32,
            )
            parts = [score[:, i * rows:(i + 1) * rows] for i in range(len(slots))]
            tops = [
                jnp.where(ok, jnp.max(part, axis=1, keepdims=True), -FAR)
                for ok, part in zip(allowed, parts)
            ]
            top = functools.reduce(jnp.maximum, tops)
            if not first:
                top = jnp.maximum(before[n], top)
            top = jnp.broadcast_to(top, (tall, HEAD_SIZE))
            weights = [
                jnp.exp2(part - jnp.where(ok, top, FAR))
                for ok, part in zip(allowed, parts)
            ]
            total = functools.reduce(jnp.add, weights)
            weight = jnp.concatenate([w.astype(jnp.bfloat16) for w in weights], axis=1)
            acc = jnp.dot(weight, vals, preferred_element_type=jnp.float32)
            if not first:
                fade = jnp.exp2(before[n] - top)
                total = total + tot_old[n] * fade
                acc = acc + acc_old[n] * fade
            done.append((top, total, acc))
        if not last:
            for n, g in enumerate(tiles):
                keep(top_s, g, done[n][0])
                keep(tot_s, g, done[n][1])
                keep(acc_s, g, done[n][2])
            return
        lane = lax.broadcasted_iota(jnp.int32, (rows, HEAD_SIZE), 1)
        sums = ltm_s[...]
        for n, g in enumerate(tiles):
            top, total, acc = done[n]
            full = jnp.sum(total, axis=1, keepdims=True)
            attended = acc / full
            log_total = top * LN2 + jnp.log(full)
            for t in range(tile):
                j = base + g + t
                cut = slice(t * rows, (t + 1) * rows)
                cols = pl.ds(pl.multiple_of(j * HEAD_SIZE, HEAD_SIZE), HEAD_SIZE)
                out_ref[:, cols] = (gate_s[:, cols] * attended[cut]).astype(out_ref.dtype)
                sums = jnp.where(lane == j, log_total[cut], sums)
        ltm_s[...] = sums

    for copy in own_q:
        copy.wait()
    for copy in own_small:
        copy.wait()

    def own(head, carry):
        visit([me], head, True, False)
        return carry

    lax.fori_loop(0, kv_heads, own, 0)
    gate_row = gate_ref[pl.ds(0, 1), :]
    for i in range(1, gate_ref.shape[0]):
        gate_row = jnp.where(sec_ref[pair] == i, gate_ref[pl.ds(i, 1), :], gate_row)
    gate_s[...] = gate_row
    ltm_s[...] = jnp.zeros_like(ltm_s)

    def step(i, carry):
        behind = me - 2 * i
        across = partner - 2 * (i - 1)

        def at_head(c, inner):
            k_on(behind, c).wait_recv()

            @pl.when(has_next)
            def _():
                k_on(behind, c).start()

            k_over(behind, c).start()
            v_on(behind, c).wait_recv()

            @pl.when(has_next)
            def _():
                v_on(behind, c).start()

            @pl.when(behind >= 2)
            def _():
                v_over(behind, c).start()

            k_over(across, c).wait_recv()
            v_over(across, c).wait_recv()
            visit([behind, across], c, False, False)
            return inner

        return lax.fori_loop(0, kv_heads, at_head, carry)

    lax.fori_loop(1, pair + 1, step, 0)

    far = 1 - side

    def end(c, carry):
        v_on(far, c).wait_recv()

        @pl.when(has_next)
        def _():
            v_on(far, c).start()

        k_over(far, c).wait_recv()
        visit([far], c, False, True)
        return carry

    lax.fori_loop(0, kv_heads, end, 0)
    lt_ref[...] = jnp.transpose(ltm_s[...])[:q_heads]

    def settle(i, carry):
        slot = me - 2 * i
        for c in range(chunks):

            @pl.when(has_next)
            def _():
                k_on(slot, c).wait_send()
                v_on(slot, c).wait_send()

            k_over(slot, c).wait_send()

            @pl.when((slot >= 2) | (i == 0))
            def _():
                v_over(slot, c).wait_send()

        return carry

    lax.fori_loop(0, pair + 1, settle, 0)

    @pl.when(has_next)
    def _():
        for c in range(chunks):
            v_on(far, c).wait_send()


def solution(mesh):
    count = mesh.shape["tm"]

    def on_device(queries, keys, values, span_mask, section, section_gate):
        rows = queries.shape[0]
        q_heads = queries.shape[1] // HEAD_SIZE
        kv_heads = keys.shape[1] // HEAD_SIZE
        assert CH == 2 * rows and count % 2 == 0
        chunks = kv_heads
        vmem = pl.BlockSpec(memory_space=pltpu.VMEM)
        dma = pltpu.SemaphoreType.DMA
        state = pltpu.VMEM((q_heads, rows, HEAD_SIZE), jnp.float32)
        held = pltpu.VMEM((count, kv_heads, rows, HEAD_SIZE), jnp.bfloat16)
        return pl.pallas_call(
            functools.partial(kernel, count, chunks),
            out_shape=(
                pltpu.VMEM(queries.shape, jnp.bfloat16),
                pltpu.VMEM((q_heads, rows), jnp.float32),
            ),
            in_specs=[pl.BlockSpec(memory_space=pltpu.HBM)] * 6,
            out_specs=(vmem, vmem),
            scratch_shapes=[
                pltpu.VMEM((q_heads, rows, HEAD_SIZE), jnp.bfloat16),
                held, held, state, state, state,
                pltpu.VMEM((rows, HEAD_SIZE), jnp.float32),
                pltpu.VMEM((1, queries.shape[1]), jnp.float32),
                pltpu.SMEM(span_mask.shape, jnp.int32),
                pltpu.SMEM(section.shape, jnp.int32),
                pltpu.VMEM(section_gate.shape, jnp.float32),
                dma((3,)), dma((q_heads,)), dma((kv_heads,)), dma((kv_heads,)),
            ] + [dma((count, chunks))] * 6,
            compiler_params=pltpu.CompilerParams(
                collective_id=0, has_side_effects=True, vmem_limit_bytes=60*2**20
            ),
            name="span_attention",
        )(queries, keys, values, span_mask, section, section_gate)

    placed = (
        P(("grp", "tm"), "head"),
        P(("grp", "tm"), "head"),
        P(("grp", "tm"), "head"),
        P("grp", None),
        P("grp"),
        P(None, "head"),
    )
    return jax.shard_map(
        on_device,
        mesh=mesh,
        in_specs=placed,
        out_specs=(P(("grp", "tm"), "head"), P("head", ("grp", "tm"))),
        check_vma=False,
    )
```

```python
import functools
import math

import jax
import jax.numpy as jnp
from jax import lax
from jax.experimental import pallas as pl
from jax.experimental.pallas import tpu as pltpu
from jax.sharding import PartitionSpec as P

HEAD_SIZE = 128
CH = 256
MESH = pl.DeviceIdType.MESH
LOG2E = 1.4426950408889634
LN2 = 0.6931471805599453
FAR = 1e30


def kernel(
    count, chunks, q_hbm, k_hbm, v_hbm, mask_hbm, sec_hbm, gate_hbm, out_ref, lt_ref,
    qbuf, kbuf, vbuf, top_s, tot_s, acc_s, ltm_s, gate_s, mask_ref, sec_ref, gate_ref, small, qsem, ksem, vsem,
    krecv, vrecv, kz, vz, ky, vy,
):
    q_heads, rows = qbuf.shape[0], qbuf.shape[1]
    kv_heads = kbuf.shape[1]
    group = q_heads // kv_heads
    per = kv_heads // chunks
    pairs = count // 2
    tile = group
    factor = LOG2E / math.sqrt(HEAD_SIZE)

    me = lax.axis_index("tm")
    pair = me // 2
    side = me % 2
    partner = me + 1 - 2 * side
    has_prev = pair > 0
    has_next = pair < pairs - 1

    barrier = pltpu.get_barrier_semaphore()
    pl.semaphore_signal(barrier, inc=1, device_id={"tm": partner}, device_id_type=MESH)

    @pl.when(has_next)
    def _():
        pl.semaphore_signal(barrier, inc=1, device_id={"tm": me + 2}, device_id_type=MESH)

    @pl.when(has_prev)
    def _():
        pl.semaphore_signal(barrier, inc=1, device_id={"tm": me - 2}, device_id_type=MESH)

    pl.semaphore_wait(
        barrier, 1 + has_next.astype(jnp.int32) + has_prev.astype(jnp.int32)
    )

    def send(buf, send_sem, recv_sem, slot, c, target):
        piece = buf.at[slot, pl.ds(c * per, per)]
        return pltpu.make_async_remote_copy(
            src_ref=piece,
            dst_ref=piece,
            send_sem=send_sem.at[slot, c],
            recv_sem=recv_sem.at[slot, c],
            device_id={"tm": target},
            device_id_type=MESH,
        )

    def k_on(slot, c):
        return send(kbuf, kz, krecv, slot, c, me + 2)

    def v_on(slot, c):
        return send(vbuf, vz, vrecv, slot, c, me + 2)

    def k_over(slot, c):
        return send(kbuf, ky, krecv, slot, c, partner)

    def v_over(slot, c):
        return send(vbuf, vy, vrecv, slot, c, partner)

    def first_send(src, buf, send_sem, recv_sem, c, target):
        return pltpu.make_async_remote_copy(
            src_ref=src.at[:, pl.ds(c * HEAD_SIZE, HEAD_SIZE)],
            dst_ref=buf.at[me, c],
            send_sem=send_sem.at[me, c],
            recv_sem=recv_sem.at[me, c],
            device_id={"tm": target},
            device_id_type=MESH,
        )

    for c in range(kv_heads):

        @pl.when(has_next)
        def _():
            first_send(k_hbm, kbuf, kz, krecv, c, me + 2).start()

        first_send(k_hbm, kbuf, ky, krecv, c, partner).start()

        @pl.when(has_next)
        def _():
            first_send(v_hbm, vbuf, vz, vrecv, c, me + 2).start()

        first_send(v_hbm, vbuf, vy, vrecv, c, partner).start()

    def head_copy(src, dst, sem, head):
        return pltpu.make_async_copy(
            src.at[:, pl.ds(head * HEAD_SIZE, HEAD_SIZE)], dst, sem
        )

    own_k = [head_copy(k_hbm, kbuf.at[me, h], ksem.at[h], h) for h in range(kv_heads)]
    own_v = [head_copy(v_hbm, vbuf.at[me, h], vsem.at[h], h) for h in range(kv_heads)]
    own_q = [head_copy(q_hbm, qbuf.at[h], qsem.at[h], h) for h in range(q_heads)]
    own_small = [
        pltpu.make_async_copy(mask_hbm, mask_ref, small.at[0]),
        pltpu.make_async_copy(sec_hbm, sec_ref, small.at[1]),
        pltpu.make_async_copy(gate_hbm, gate_ref, small.at[2]),
    ]
    own_all = own_small + own_k + own_v + own_q
    for copy in own_all:
        copy.start()

    def visit(slots, head, first, last):
        allowed = [mask_ref[pair, slot // 2] > 0 for slot in slots]
        keys = jnp.concatenate([kbuf[slot, head] for slot in slots], axis=0)
        vals = jnp.concatenate([vbuf[slot, head] for slot in slots], axis=0)
        base = head * group
        tiles = range(0, group, tile)
        tall = tile * rows

        def held(ref, g):
            return ref[pl.ds(base + g, tile)].reshape(tall, HEAD_SIZE)

        def keep(ref, g, value):
            ref[pl.ds(base + g, tile)] = value.reshape(tile, rows, HEAD_SIZE)

        if not first:
            before = [held(top_s, g) for g in tiles]
            tot_old = [held(tot_s, g) for g in tiles]
            acc_old = [held(acc_s, g) for g in tiles]
        done = []
        for n, g in enumerate(tiles):
            score = factor * lax.dot_general(
                held(qbuf, g), keys, (((1,), (1,)), ((), ())),
                preferred_element_type=jnp.float32,
            )
            parts = [score[:, i * rows:(i + 1) * rows] for i in range(len(slots))]
            tops = [
                jnp.where(ok, jnp.max(part, axis=1, keepdims=True), -FAR)
                for ok, part in zip(allowed, parts)
            ]
            top = functools.reduce(jnp.maximum, tops)
            if not first:
                top = jnp.maximum(before[n], top)
            top = jnp.broadcast_to(top, (tall, HEAD_SIZE))
            weights = [
                jnp.exp2(part - jnp.where(ok, top, FAR))
                for ok, part in zip(allowed, parts)
            ]
            total = functools.reduce(jnp.add, weights)
            weight = jnp.concatenate([w.astype(jnp.bfloat16) for w in weights], axis=1)
            acc = jnp.dot(weight, vals, preferred_element_type=jnp.float32)
            if not first:
                fade = jnp.exp2(before[n] - top)
                total = total + tot_old[n] * fade
                acc = acc + acc_old[n] * fade
            done.append((top, total, acc))
        if not last:
            for n, g in enumerate(tiles):
                keep(top_s, g, done[n][0])
                keep(tot_s, g, done[n][1])
                keep(acc_s, g, done[n][2])
            return
        lane = lax.broadcasted_iota(jnp.int32, (rows, HEAD_SIZE), 1)
        sums = ltm_s[...]
        for n, g in enumerate(tiles):
            top, total, acc = done[n]
            full = jnp.sum(total, axis=1, keepdims=True)
            attended = acc / full
            log_total = top * LN2 + jnp.log(full)
            for t in range(tile):
                j = base + g + t
                cut = slice(t * rows, (t + 1) * rows)
                cols = pl.ds(pl.multiple_of(j * HEAD_SIZE, HEAD_SIZE), HEAD_SIZE)
                out_ref[:, cols] = (gate_s[:, cols] * attended[cut]).astype(out_ref.dtype)
                sums = jnp.where(lane == j, log_total[cut], sums)
        ltm_s[...] = sums

    for copy in own_all:
        copy.wait()

    def own(head, carry):
        visit([me], head, True, False)
        return carry

    lax.fori_loop(0, kv_heads, own, 0)
    gate_row = gate_ref[pl.ds(0, 1), :]
    for i in range(1, gate_ref.shape[0]):
        gate_row = jnp.where(sec_ref[pair] == i, gate_ref[pl.ds(i, 1), :], gate_row)
    gate_s[...] = gate_row
    ltm_s[...] = jnp.zeros_like(ltm_s)

    def step(i, carry):
        behind = me - 2 * i
        across = partner - 2 * (i - 1)

        def at_head(c, inner):
            k_on(behind, c).wait_recv()

            @pl.when(has_next)
            def _():
                k_on(behind, c).start()

            k_over(behind, c).start()
            v_on(behind, c).wait_recv()

            @pl.when(has_next)
            def _():
                v_on(behind, c).start()

            @pl.when(behind >= 2)
            def _():
                v_over(behind, c).start()

            k_over(across, c).wait_recv()
            v_over(across, c).wait_recv()
            visit([behind, across], c, False, False)
            return inner

        return lax.fori_loop(0, kv_heads, at_head, carry)

    lax.fori_loop(1, pair + 1, step, 0)

    far = 1 - side

    def end(c, carry):
        v_on(far, c).wait_recv()

        @pl.when(has_next)
        def _():
            v_on(far, c).start()

        k_over(far, c).wait_recv()
        visit([far], c, False, True)
        return carry

    lax.fori_loop(0, kv_heads, end, 0)
    lt_ref[...] = jnp.transpose(ltm_s[...])[:q_heads]

    for c in range(kv_heads):

        @pl.when(has_next)
        def _():
            first_send(k_hbm, kbuf, kz, krecv, c, me + 2).wait_send()
            first_send(v_hbm, vbuf, vz, vrecv, c, me + 2).wait_send()

        first_send(k_hbm, kbuf, ky, krecv, c, partner).wait_send()
        first_send(v_hbm, vbuf, vy, vrecv, c, partner).wait_send()

    def settle(i, carry):
        slot = me - 2 * i
        for c in range(chunks):

            @pl.when(has_next)
            def _():
                k_on(slot, c).wait_send()
                v_on(slot, c).wait_send()

            k_over(slot, c).wait_send()

            @pl.when(slot >= 2)
            def _():
                v_over(slot, c).wait_send()

        return carry

    lax.fori_loop(1, pair + 1, settle, 0)

    @pl.when(has_next)
    def _():
        for c in range(chunks):
            v_on(far, c).wait_send()


def finish(mixed_ref, log_ref, mixed_out, log_out, sem):
    parts = sem.shape[0] - 1
    high = mixed_ref.shape[0] // parts
    copies = [
        pltpu.make_async_copy(
            mixed_ref.at[pl.ds(i * high, high)],
            mixed_out.at[pl.ds(i * high, high)],
            sem.at[i],
        )
        for i in range(parts)
    ] + [pltpu.make_async_copy(log_ref, log_out, sem.at[parts])]
    for copy in copies:
        copy.start()
    for copy in copies:
        copy.wait()


def solution(mesh):
    count = mesh.shape["tm"]

    def on_device(queries, keys, values, span_mask, section, section_gate):
        rows = queries.shape[0]
        q_heads = queries.shape[1] // HEAD_SIZE
        kv_heads = keys.shape[1] // HEAD_SIZE
        assert CH == 2 * rows and count % 2 == 0
        chunks = kv_heads
        vmem = pl.BlockSpec(memory_space=pltpu.VMEM)
        dma = pltpu.SemaphoreType.DMA
        keep_near = lambda x: pltpu.with_memory_space_constraint(x, pltpu.VMEM)
        state = pltpu.VMEM((q_heads, rows, HEAD_SIZE), jnp.float32)
        held = pltpu.VMEM((count, kv_heads, rows, HEAD_SIZE), jnp.bfloat16)
        mixed, log_total = pl.pallas_call(
            functools.partial(kernel, count, chunks),
            out_shape=(
                pltpu.VMEM(queries.shape, jnp.bfloat16),
                pltpu.VMEM((q_heads, rows), jnp.float32),
            ),
            in_specs=[pl.BlockSpec(memory_space=pltpu.HBM)] * 6,
            out_specs=(vmem, vmem),
            scratch_shapes=[
                pltpu.VMEM((q_heads, rows, HEAD_SIZE), jnp.bfloat16),
                held, held, state, state, state,
                pltpu.VMEM((rows, HEAD_SIZE), jnp.float32),
                pltpu.VMEM((1, queries.shape[1]), jnp.float32),
                pltpu.SMEM(span_mask.shape, jnp.int32),
                pltpu.SMEM(section.shape, jnp.int32),
                pltpu.VMEM(section_gate.shape, jnp.float32),
                dma((3,)), dma((q_heads,)), dma((kv_heads,)), dma((kv_heads,)),
            ] + [dma((count, chunks))] * 6,
            compiler_params=pltpu.CompilerParams(
                collective_id=0, has_side_effects=True, vmem_limit_bytes=60*2**20
            ),
            name="span_attention",
        )(queries, keys, values, span_mask, section, section_gate)
        return pl.pallas_call(
            finish,
            out_shape=(
                jax.ShapeDtypeStruct(mixed.shape, mixed.dtype),
                jax.ShapeDtypeStruct(log_total.shape, log_total.dtype),
            ),
            in_specs=[vmem, vmem],
            out_specs=[pl.BlockSpec(memory_space=pltpu.HBM)] * 2,
            scratch_shapes=[dma((5,))],
            compiler_params=pltpu.CompilerParams(vmem_limit_bytes=4 * 2**20),
            name="write_back",
        )(keep_near(mixed), keep_near(log_total))

    placed = (
        P(("grp", "tm"), "head"),
        P(("grp", "tm"), "head"),
        P(("grp", "tm"), "head"),
        P("grp", None),
        P("grp"),
        P(None, "head"),
    )
    return jax.shard_map(
        on_device,
        mesh=mesh,
        in_specs=placed,
        out_specs=(P(("grp", "tm"), "head"), P("head", ("grp", "tm"))),
        check_vma=False,
    )
```

```python
import functools
import math

import jax
import jax.numpy as jnp
from jax import lax
from jax.experimental import pallas as pl
from jax.experimental.pallas import tpu as pltpu
from jax.sharding import PartitionSpec as P

HEAD_SIZE = 128
CH = 256
MESH = pl.DeviceIdType.MESH
LOG2E = 1.4426950408889634
LN2 = 0.6931471805599453
FAR = 1e30


def kernel(
    count, chunks, q_hbm, k_hbm, v_hbm, mask_hbm, sec_hbm, gate_hbm, out_ref, lt_ref,
    qbuf, kbuf, vbuf, top_s, tot_s, acc_s, ltm_s, gate_s, mask_ref, sec_ref, gate_ref, small, qsem, ksem, vsem,
    krecv, vrecv, kz, vz, ky, vy,
):
    q_heads, rows = qbuf.shape[0], qbuf.shape[1]
    kv_heads = kbuf.shape[1]
    group = q_heads // kv_heads
    per = kv_heads // chunks
    pairs = count // 2
    tile = group
    factor = LOG2E / math.sqrt(HEAD_SIZE)

    me = lax.axis_index("tm")
    pair = me // 2
    side = me % 2
    partner = me + 1 - 2 * side
    has_prev = pair > 0
    has_next = pair < pairs - 1

    barrier = pltpu.get_barrier_semaphore()
    pl.semaphore_signal(barrier, inc=1, device_id={"tm": partner}, device_id_type=MESH)

    @pl.when(has_next)
    def _():
        pl.semaphore_signal(barrier, inc=1, device_id={"tm": me + 2}, device_id_type=MESH)

    @pl.when(has_prev)
    def _():
        pl.semaphore_signal(barrier, inc=1, device_id={"tm": me - 2}, device_id_type=MESH)

    pl.semaphore_wait(
        barrier, 1 + has_next.astype(jnp.int32) + has_prev.astype(jnp.int32)
    )

    def send(buf, send_sem, recv_sem, slot, c, target):
        piece = buf.at[slot, pl.ds(c * per, per)]
        return pltpu.make_async_remote_copy(
            src_ref=piece,
            dst_ref=piece,
            send_sem=send_sem.at[slot, c],
            recv_sem=recv_sem.at[slot, c],
            device_id={"tm": target},
            device_id_type=MESH,
        )

    def k_on(slot, c):
        return send(kbuf, kz, krecv, slot, c, me + 2)

    def v_on(slot, c):
        return send(vbuf, vz, vrecv, slot, c, me + 2)

    def k_over(slot, c):
        return send(kbuf, ky, krecv, slot, c, partner)

    def v_over(slot, c):
        return send(vbuf, vy, vrecv, slot, c, partner)

    def first_send(src, buf, send_sem, recv_sem, c, target):
        return pltpu.make_async_remote_copy(
            src_ref=src.at[:, pl.ds(c * HEAD_SIZE, HEAD_SIZE)],
            dst_ref=buf.at[me, c],
            send_sem=send_sem.at[me, c],
            recv_sem=recv_sem.at[me, c],
            device_id={"tm": target},
            device_id_type=MESH,
        )

    for c in range(kv_heads):

        @pl.when(has_next)
        def _():
            first_send(k_hbm, kbuf, kz, krecv, c, me + 2).start()

        first_send(k_hbm, kbuf, ky, krecv, c, partner).start()

    for c in range(kv_heads):

        @pl.when(has_next)
        def _():
            first_send(v_hbm, vbuf, vz, vrecv, c, me + 2).start()

        first_send(v_hbm, vbuf, vy, vrecv, c, partner).start()

    def head_copy(src, dst, sem, head):
        return pltpu.make_async_copy(
            src.at[:, pl.ds(head * HEAD_SIZE, HEAD_SIZE)], dst, sem
        )

    own_k = [head_copy(k_hbm, kbuf.at[me, h], ksem.at[h], h) for h in range(kv_heads)]
    own_v = [head_copy(v_hbm, vbuf.at[me, h], vsem.at[h], h) for h in range(kv_heads)]
    own_q = [head_copy(q_hbm, qbuf.at[h], qsem.at[h], h) for h in range(q_heads)]
    own_small = [
        pltpu.make_async_copy(mask_hbm, mask_ref, small.at[0]),
        pltpu.make_async_copy(sec_hbm, sec_ref, small.at[1]),
        pltpu.make_async_copy(gate_hbm, gate_ref, small.at[2]),
    ]
    own_all = own_small + own_k + own_v + own_q
    for copy in own_all:
        copy.start()

    def visit(slots, head, first, last):
        allowed = [mask_ref[pair, slot // 2] > 0 for slot in slots]
        keys = jnp.concatenate([kbuf[slot, head] for slot in slots], axis=0)
        vals = jnp.concatenate([vbuf[slot, head] for slot in slots], axis=0)
        base = head * group
        tiles = range(0, group, tile)
        tall = tile * rows

        def held(ref, g):
            return ref[pl.ds(base + g, tile)].reshape(tall, HEAD_SIZE)

        def keep(ref, g, value):
            ref[pl.ds(base + g, tile)] = value.reshape(tile, rows, HEAD_SIZE)

        if not first:
            before = [held(top_s, g) for g in tiles]
            tot_old = [held(tot_s, g) for g in tiles]
            acc_old = [held(acc_s, g) for g in tiles]
        done = []
        for n, g in enumerate(tiles):
            score = factor * lax.dot_general(
                held(qbuf, g), keys, (((1,), (1,)), ((), ())),
                preferred_element_type=jnp.float32,
            )
            parts = [score[:, i * rows:(i + 1) * rows] for i in range(len(slots))]
            tops = [
                jnp.where(ok, jnp.max(part, axis=1, keepdims=True), -FAR)
                for ok, part in zip(allowed, parts)
            ]
            top = functools.reduce(jnp.maximum, tops)
            if not first:
                top = jnp.maximum(before[n], top)
            top = jnp.broadcast_to(top, (tall, HEAD_SIZE))
            weights = [
                jnp.exp2(part - jnp.where(ok, top, FAR))
                for ok, part in zip(allowed, parts)
            ]
            total = functools.reduce(jnp.add, weights)
            weight = jnp.concatenate([w.astype(jnp.bfloat16) for w in weights], axis=1)
            acc = jnp.dot(weight, vals, preferred_element_type=jnp.float32)
            if not first:
                fade = jnp.exp2(before[n] - top)
                total = total + tot_old[n] * fade
                acc = acc + acc_old[n] * fade
            done.append((top, total, acc))
        if not last:
            for n, g in enumerate(tiles):
                keep(top_s, g, done[n][0])
                keep(tot_s, g, done[n][1])
                keep(acc_s, g, done[n][2])
            return
        lane = lax.broadcasted_iota(jnp.int32, (rows, HEAD_SIZE), 1)
        sums = ltm_s[...]
        for n, g in enumerate(tiles):
            top, total, acc = done[n]
            full = jnp.sum(total, axis=1, keepdims=True)
            attended = acc / full
            log_total = top * LN2 + jnp.log(full)
            for t in range(tile):
                j = base + g + t
                cut = slice(t * rows, (t + 1) * rows)
                cols = pl.ds(pl.multiple_of(j * HEAD_SIZE, HEAD_SIZE), HEAD_SIZE)
                out_ref[:, cols] = (gate_s[:, cols] * attended[cut]).astype(out_ref.dtype)
                sums = jnp.where(lane == j, log_total[cut], sums)
        ltm_s[...] = sums

    for copy in own_all:
        copy.wait()

    def own(head, carry):
        visit([me], head, True, False)
        return carry

    lax.fori_loop(0, kv_heads, own, 0)
    gate_row = gate_ref[pl.ds(0, 1), :]
    for i in range(1, gate_ref.shape[0]):
        gate_row = jnp.where(sec_ref[pair] == i, gate_ref[pl.ds(i, 1), :], gate_row)
    gate_s[...] = gate_row
    ltm_s[...] = jnp.zeros_like(ltm_s)

    def step(i, carry):
        behind = me - 2 * i
        across = partner - 2 * (i - 1)

        def pass_keys(c, inner):
            k_on(behind, c).wait_recv()

            @pl.when(has_next)
            def _():
                k_on(behind, c).start()

            k_over(behind, c).start()
            return inner

        lax.fori_loop(0, kv_heads, pass_keys, 0)

        def at_head(c, inner):
            v_on(behind, c).wait_recv()

            @pl.when(has_next)
            def _():
                v_on(behind, c).start()

            @pl.when(behind >= 2)
            def _():
                v_over(behind, c).start()

            k_over(across, c).wait_recv()
            v_over(across, c).wait_recv()
            visit([behind, across], c, False, False)
            return inner

        return lax.fori_loop(0, kv_heads, at_head, carry)

    lax.fori_loop(1, pair + 1, step, 0)

    far = 1 - side

    def end(c, carry):
        v_on(far, c).wait_recv()

        @pl.when(has_next)
        def _():
            v_on(far, c).start()

        k_over(far, c).wait_recv()
        visit([far], c, False, True)
        return carry

    lax.fori_loop(0, kv_heads, end, 0)
    lt_ref[...] = jnp.transpose(ltm_s[...])[:q_heads]

    for c in range(kv_heads):

        @pl.when(has_next)
        def _():
            first_send(k_hbm, kbuf, kz, krecv, c, me + 2).wait_send()
            first_send(v_hbm, vbuf, vz, vrecv, c, me + 2).wait_send()

        first_send(k_hbm, kbuf, ky, krecv, c, partner).wait_send()
        first_send(v_hbm, vbuf, vy, vrecv, c, partner).wait_send()

    def settle(i, carry):
        slot = me - 2 * i
        for c in range(chunks):

            @pl.when(has_next)
            def _():
                k_on(slot, c).wait_send()
                v_on(slot, c).wait_send()

            k_over(slot, c).wait_send()

            @pl.when(slot >= 2)
            def _():
                v_over(slot, c).wait_send()

        return carry

    lax.fori_loop(1, pair + 1, settle, 0)

    @pl.when(has_next)
    def _():
        for c in range(chunks):
            v_on(far, c).wait_send()


def finish(mixed_ref, log_ref, mixed_out, log_out, sem):
    parts = sem.shape[0] - 1
    high = mixed_ref.shape[0] // parts
    copies = [
        pltpu.make_async_copy(
            mixed_ref.at[pl.ds(i * high, high)],
            mixed_out.at[pl.ds(i * high, high)],
            sem.at[i],
        )
        for i in range(parts)
    ] + [pltpu.make_async_copy(log_ref, log_out, sem.at[parts])]
    for copy in copies:
        copy.start()
    for copy in copies:
        copy.wait()


def solution(mesh):
    count = mesh.shape["tm"]

    def on_device(queries, keys, values, span_mask, section, section_gate):
        rows = queries.shape[0]
        q_heads = queries.shape[1] // HEAD_SIZE
        kv_heads = keys.shape[1] // HEAD_SIZE
        assert CH == 2 * rows and count % 2 == 0
        chunks = kv_heads
        vmem = pl.BlockSpec(memory_space=pltpu.VMEM)
        dma = pltpu.SemaphoreType.DMA
        keep_near = lambda x: pltpu.with_memory_space_constraint(x, pltpu.VMEM)
        state = pltpu.VMEM((q_heads, rows, HEAD_SIZE), jnp.float32)
        held = pltpu.VMEM((count, kv_heads, rows, HEAD_SIZE), jnp.bfloat16)
        mixed, log_total = pl.pallas_call(
            functools.partial(kernel, count, chunks),
            out_shape=(
                pltpu.VMEM(queries.shape, jnp.bfloat16),
                pltpu.VMEM((q_heads, rows), jnp.float32),
            ),
            in_specs=[pl.BlockSpec(memory_space=pltpu.HBM)] * 6,
            out_specs=(vmem, vmem),
            scratch_shapes=[
                pltpu.VMEM((q_heads, rows, HEAD_SIZE), jnp.bfloat16),
                held, held, state, state, state,
                pltpu.VMEM((rows, HEAD_SIZE), jnp.float32),
                pltpu.VMEM((1, queries.shape[1]), jnp.float32),
                pltpu.SMEM(span_mask.shape, jnp.int32),
                pltpu.SMEM(section.shape, jnp.int32),
                pltpu.VMEM(section_gate.shape, jnp.float32),
                dma((3,)), dma((q_heads,)), dma((kv_heads,)), dma((kv_heads,)),
            ] + [dma((count, chunks))] * 6,
            compiler_params=pltpu.CompilerParams(
                collective_id=0, has_side_effects=True, vmem_limit_bytes=60*2**20
            ),
            name="span_attention",
        )(queries, keys, values, span_mask, section, section_gate)
        return pl.pallas_call(
            finish,
            out_shape=(
                jax.ShapeDtypeStruct(mixed.shape, mixed.dtype),
                jax.ShapeDtypeStruct(log_total.shape, log_total.dtype),
            ),
            in_specs=[vmem, vmem],
            out_specs=[pl.BlockSpec(memory_space=pltpu.HBM)] * 2,
            scratch_shapes=[dma((5,))],
            compiler_params=pltpu.CompilerParams(vmem_limit_bytes=4 * 2**20),
            name="write_back",
        )(keep_near(mixed), keep_near(log_total))

    placed = (
        P(("grp", "tm"), "head"),
        P(("grp", "tm"), "head"),
        P(("grp", "tm"), "head"),
        P("grp", None),
        P("grp"),
        P(None, "head"),
    )
    return jax.shard_map(
        on_device,
        mesh=mesh,
        in_specs=placed,
        out_specs=(P(("grp", "tm"), "head"), P("head", ("grp", "tm"))),
        check_vma=False,
    )
```

```python
import functools
import math

import jax
import jax.numpy as jnp
from jax import lax
from jax.experimental import pallas as pl
from jax.experimental.pallas import tpu as pltpu
from jax.sharding import PartitionSpec as P

HEAD_SIZE = 128
CH = 256
MESH = pl.DeviceIdType.MESH
LOG2E = 1.4426950408889634
LN2 = 0.6931471805599453
FAR = 1e30


def kernel(
    count, chunks, q_hbm, k_hbm, v_hbm, mask_hbm, sec_hbm, gate_hbm, out_ref, lt_ref,
    qbuf, kbuf, vbuf, top_s, tot_s, acc_s, ltm_s, gate_s, mask_ref, sec_ref, gate_ref, small, qsem, ksem, vsem,
    krecv, vrecv, kz, vz, ky, vy,
):
    q_heads, rows = qbuf.shape[0], qbuf.shape[1]
    kv_heads = kbuf.shape[1]
    group = q_heads // kv_heads
    per = kv_heads // chunks
    pairs = count // 2
    tile = group
    factor = LOG2E / math.sqrt(HEAD_SIZE)

    me = lax.axis_index("tm")
    pair = me // 2
    side = me % 2
    partner = me + 1 - 2 * side
    has_prev = pair > 0
    has_next = pair < pairs - 1

    barrier = pltpu.get_barrier_semaphore()
    pl.semaphore_signal(barrier, inc=1, device_id={"tm": partner}, device_id_type=MESH)

    @pl.when(has_next)
    def _():
        pl.semaphore_signal(barrier, inc=1, device_id={"tm": me + 2}, device_id_type=MESH)

    @pl.when(has_prev)
    def _():
        pl.semaphore_signal(barrier, inc=1, device_id={"tm": me - 2}, device_id_type=MESH)

    pl.semaphore_wait(
        barrier, 1 + has_next.astype(jnp.int32) + has_prev.astype(jnp.int32)
    )

    def send(buf, send_sem, recv_sem, slot, c, target):
        piece = buf.at[slot, pl.ds(c * per, per)]
        return pltpu.make_async_remote_copy(
            src_ref=piece,
            dst_ref=piece,
            send_sem=send_sem.at[slot, c],
            recv_sem=recv_sem.at[slot, c],
            device_id={"tm": target},
            device_id_type=MESH,
        )

    def k_on(slot, c):
        return send(kbuf, kz, krecv, slot, c, me + 2)

    def v_on(slot, c):
        return send(vbuf, vz, vrecv, slot, c, me + 2)

    def k_over(slot, c):
        return send(kbuf, ky, krecv, slot, c, partner)

    def v_over(slot, c):
        return send(vbuf, vy, vrecv, slot, c, partner)

    def first_send(src, buf, send_sem, recv_sem, c, target):
        return pltpu.make_async_remote_copy(
            src_ref=src.at[:, pl.ds(c * HEAD_SIZE, HEAD_SIZE)],
            dst_ref=buf.at[me, c],
            send_sem=send_sem.at[me, c],
            recv_sem=recv_sem.at[me, c],
            device_id={"tm": target},
            device_id_type=MESH,
        )

    for c in range(kv_heads):

        @pl.when(has_next)
        def _():
            first_send(k_hbm, kbuf, kz, krecv, c, me + 2).start()

        first_send(k_hbm, kbuf, ky, krecv, c, partner).start()

    for c in range(kv_heads):

        @pl.when(has_next)
        def _():
            first_send(v_hbm, vbuf, vz, vrecv, c, me + 2).start()

        first_send(v_hbm, vbuf, vy, vrecv, c, partner).start()

    def head_copy(src, dst, sem, head):
        return pltpu.make_async_copy(
            src.at[:, pl.ds(head * HEAD_SIZE, HEAD_SIZE)], dst, sem
        )

    own_k = [head_copy(k_hbm, kbuf.at[me, h], ksem.at[h], h) for h in range(kv_heads)]
    own_v = [head_copy(v_hbm, vbuf.at[me, h], vsem.at[h], h) for h in range(kv_heads)]
    own_q = [head_copy(q_hbm, qbuf.at[h], qsem.at[h], h) for h in range(q_heads)]
    own_small = [
        pltpu.make_async_copy(mask_hbm, mask_ref, small.at[0]),
        pltpu.make_async_copy(sec_hbm, sec_ref, small.at[1]),
        pltpu.make_async_copy(gate_hbm, gate_ref, small.at[2]),
    ]
    own_all = own_small + own_k + own_v + own_q
    for copy in own_all:
        copy.start()

    def visit(slots, head, first, last):
        allowed = [mask_ref[pair, slot // 2] > 0 for slot in slots]
        keys = jnp.concatenate([kbuf[slot, head] for slot in slots], axis=0)
        vals = jnp.concatenate([vbuf[slot, head] for slot in slots], axis=0)
        base = head * group
        tiles = range(0, group, tile)
        tall = tile * rows

        def held(ref, g):
            return ref[pl.ds(base + g, tile)].reshape(tall, HEAD_SIZE)

        def keep(ref, g, value):
            ref[pl.ds(base + g, tile)] = value.reshape(tile, rows, HEAD_SIZE)

        if not first:
            before = [held(top_s, g) for g in tiles]
            tot_old = [held(tot_s, g) for g in tiles]
            acc_old = [held(acc_s, g) for g in tiles]
        done = []
        for n, g in enumerate(tiles):
            score = factor * lax.dot_general(
                held(qbuf, g), keys, (((1,), (1,)), ((), ())),
                preferred_element_type=jnp.float32,
            )
            parts = [score[:, i * rows:(i + 1) * rows] for i in range(len(slots))]
            tops = [
                jnp.where(ok, jnp.max(part, axis=1, keepdims=True), -FAR)
                for ok, part in zip(allowed, parts)
            ]
            top = functools.reduce(jnp.maximum, tops)
            if not first:
                top = jnp.maximum(before[n], top)
            top = jnp.broadcast_to(top, (tall, HEAD_SIZE))
            weights = [
                jnp.exp2(part - jnp.where(ok, top, FAR))
                for ok, part in zip(allowed, parts)
            ]
            total = functools.reduce(jnp.add, weights)
            weight = jnp.concatenate([w.astype(jnp.bfloat16) for w in weights], axis=1)
            acc = jnp.dot(weight, vals, preferred_element_type=jnp.float32)
            if not first:
                fade = jnp.exp2(before[n] - top)
                total = total + tot_old[n] * fade
                acc = acc + acc_old[n] * fade
            done.append((top, total, acc))
        if not last:
            for n, g in enumerate(tiles):
                keep(top_s, g, done[n][0])
                keep(tot_s, g, done[n][1])
                keep(acc_s, g, done[n][2])
            return
        lane = lax.broadcasted_iota(jnp.int32, (rows, HEAD_SIZE), 1)
        sums = ltm_s[...]
        for n, g in enumerate(tiles):
            top, total, acc = done[n]
            full = jnp.sum(total, axis=1, keepdims=True)
            attended = acc / full
            log_total = top * LN2 + jnp.log(full)
            for t in range(tile):
                j = base + g + t
                cut = slice(t * rows, (t + 1) * rows)
                cols = pl.ds(pl.multiple_of(j * HEAD_SIZE, HEAD_SIZE), HEAD_SIZE)
                out_ref[:, cols] = (gate_s[:, cols] * attended[cut]).astype(out_ref.dtype)
                sums = jnp.where(lane == j, log_total[cut], sums)
        ltm_s[...] = sums

    for copy in own_all:
        copy.wait()

    def own(head, carry):
        visit([me], head, True, False)
        return carry

    lax.fori_loop(0, kv_heads, own, 0)
    gate_row = gate_ref[pl.ds(0, 1), :]
    for i in range(1, gate_ref.shape[0]):
        gate_row = jnp.where(sec_ref[pair] == i, gate_ref[pl.ds(i, 1), :], gate_row)
    gate_s[...] = gate_row
    ltm_s[...] = jnp.zeros_like(ltm_s)

    def step(i, carry):
        behind = me - 2 * i
        across = partner - 2 * (i - 1)

        def pass_keys(c, inner):
            k_on(behind, c).wait_recv()

            @pl.when(has_next)
            def _():
                k_on(behind, c).start()

            k_over(behind, c).start()
            return inner

        lax.fori_loop(0, kv_heads, pass_keys, 0)

        def at_head(c, inner):
            v_on(behind, c).wait_recv()

            @pl.when(has_next)
            def _():
                v_on(behind, c).start()

            @pl.when(behind >= 2)
            def _():
                v_over(behind, c).start()

            k_over(across, c).wait_recv()
            v_over(across, c).wait_recv()
            visit([behind, across], c, False, False)
            return inner

        return lax.fori_loop(0, kv_heads, at_head, carry)

    lax.fori_loop(1, pair + 1, step, 0)

    far = 1 - side

    for c in range(kv_heads):

        @pl.when(has_next)
        def _():
            first_send(k_hbm, kbuf, kz, krecv, c, me + 2).wait_send()
            first_send(v_hbm, vbuf, vz, vrecv, c, me + 2).wait_send()

        first_send(k_hbm, kbuf, ky, krecv, c, partner).wait_send()
        first_send(v_hbm, vbuf, vy, vrecv, c, partner).wait_send()

    def settle(i, carry):
        slot = me - 2 * i
        for c in range(chunks):

            @pl.when(has_next)
            def _():
                k_on(slot, c).wait_send()
                v_on(slot, c).wait_send()

            k_over(slot, c).wait_send()

            @pl.when(slot >= 2)
            def _():
                v_over(slot, c).wait_send()

        return carry

    lax.fori_loop(1, pair, settle, 0)

    def end(c, carry):
        v_on(far, c).wait_recv()

        @pl.when(has_next)
        def _():
            v_on(far, c).start()

        k_over(far, c).wait_recv()
        visit([far], c, False, True)
        return carry

    lax.fori_loop(0, kv_heads, end, 0)
    lt_ref[...] = jnp.transpose(ltm_s[...])[:q_heads]

    lax.fori_loop(jnp.maximum(pair, 1), pair + 1, settle, 0)

    @pl.when(has_next)
    def _():
        for c in range(chunks):
            v_on(far, c).wait_send()


def finish(mixed_ref, log_ref, mixed_out, log_out, sem):
    parts = sem.shape[0] - 1
    high = mixed_ref.shape[0] // parts
    copies = [
        pltpu.make_async_copy(
            mixed_ref.at[pl.ds(i * high, high)],
            mixed_out.at[pl.ds(i * high, high)],
            sem.at[i],
        )
        for i in range(parts)
    ] + [pltpu.make_async_copy(log_ref, log_out, sem.at[parts])]
    for copy in copies:
        copy.start()
    for copy in copies:
        copy.wait()


def solution(mesh):
    count = mesh.shape["tm"]

    def on_device(queries, keys, values, span_mask, section, section_gate):
        rows = queries.shape[0]
        q_heads = queries.shape[1] // HEAD_SIZE
        kv_heads = keys.shape[1] // HEAD_SIZE
        assert CH == 2 * rows and count % 2 == 0
        chunks = kv_heads
        vmem = pl.BlockSpec(memory_space=pltpu.VMEM)
        dma = pltpu.SemaphoreType.DMA
        keep_near = lambda x: pltpu.with_memory_space_constraint(x, pltpu.VMEM)
        state = pltpu.VMEM((q_heads, rows, HEAD_SIZE), jnp.float32)
        held = pltpu.VMEM((count, kv_heads, rows, HEAD_SIZE), jnp.bfloat16)
        mixed, log_total = pl.pallas_call(
            functools.partial(kernel, count, chunks),
            out_shape=(
                pltpu.VMEM(queries.shape, jnp.bfloat16),
                pltpu.VMEM((q_heads, rows), jnp.float32),
            ),
            in_specs=[pl.BlockSpec(memory_space=pltpu.HBM)] * 6,
            out_specs=(vmem, vmem),
            scratch_shapes=[
                pltpu.VMEM((q_heads, rows, HEAD_SIZE), jnp.bfloat16),
                held, held, state, state, state,
                pltpu.VMEM((rows, HEAD_SIZE), jnp.float32),
                pltpu.VMEM((1, queries.shape[1]), jnp.float32),
                pltpu.SMEM(span_mask.shape, jnp.int32),
                pltpu.SMEM(section.shape, jnp.int32),
                pltpu.VMEM(section_gate.shape, jnp.float32),
                dma((3,)), dma((q_heads,)), dma((kv_heads,)), dma((kv_heads,)),
            ] + [dma((count, chunks))] * 6,
            compiler_params=pltpu.CompilerParams(
                collective_id=0, has_side_effects=True, vmem_limit_bytes=60*2**20
            ),
            name="span_attention",
        )(queries, keys, values, span_mask, section, section_gate)
        return pl.pallas_call(
            finish,
            out_shape=(
                jax.ShapeDtypeStruct(mixed.shape, mixed.dtype),
                jax.ShapeDtypeStruct(log_total.shape, log_total.dtype),
            ),
            in_specs=[vmem, vmem],
            out_specs=[pl.BlockSpec(memory_space=pltpu.HBM)] * 2,
            scratch_shapes=[dma((5,))],
            compiler_params=pltpu.CompilerParams(vmem_limit_bytes=4 * 2**20),
            name="write_back",
        )(keep_near(mixed), keep_near(log_total))

    placed = (
        P(("grp", "tm"), "head"),
        P(("grp", "tm"), "head"),
        P(("grp", "tm"), "head"),
        P("grp", None),
        P("grp"),
        P(None, "head"),
    )
    return jax.shard_map(
        on_device,
        mesh=mesh,
        in_specs=placed,
        out_specs=(P(("grp", "tm"), "head"), P("head", ("grp", "tm"))),
        check_vma=False,
    )
```
